32 devices in a mesh: dp: 8 (over z, x), tensor: 4 (over y, core).
Axes of the slice: x: 2, y: 2, z: 4, core: 2. Of those that a mesh axis runs over, the one named last changes fastest.
Arguments:
- tokens: bfloat16 [11776, 768], P(('dp', 'tensor')), may hold values from -6 to 6
- horizons: int32 [16], P('dp'), may hold values from 4 to 30, as said below
- cotangent: bfloat16 [11776, 768], P(('dp', 'tensor')), may hold values from -6 to 6
- step_number: int32 [1], replicated, may hold values from 2 to 20
- attend_in: float32 [3, 768, 768], P(None, 'dp', 'tensor'), may hold values from -0.21875 to 0.21875
- attend_out: float32 [768, 768], P('tensor', 'dp'), may hold values from -1.75 to 1.75
- project_up: float32 [768, 3072], P('dp', 'tensor'), may hold values from -0.21875 to 0.21875
- project_down: float32 [3072, 768], P('tensor', 'dp'), may hold values from -0.109375 to 0.109375
- norm_gains: float32 [2, 768], replicated, may hold values from 0.1 to 1.9
- norm_biases: float32 [2, 768], replicated, may hold values from -1.8 to 1.8
- first_attend_in: float32 [3, 768, 768], P(None, 'dp', 'tensor'), may hold values from -0.0002480802 to 0.0002480802
- first_attend_out: float32 [768, 768], P('tensor', 'dp'), may hold values from -0.0002480802 to 0.0002480802
- first_project_up: float32 [768, 3072], P('dp', 'tensor'), may hold values from -0.0002480802 to 0.0002480802
- first_project_down: float32 [3072, 768], P('tensor', 'dp'), may hold values from -0.0002480802 to 0.0002480802
- first_norms: float32 [4, 768], P(None, 'dp'), may hold values from -0.0007442406 to 0.0007442406
- second_attend_in: float32 [3, 768, 768], P(None, 'dp', 'tensor'), may hold values from 7.064254e-09 to 2.8257016e-08
- second_attend_out: float32 [768, 768], P('tensor', 'dp'), may hold values from 7.064254e-09 to 2.8257016e-08
- second_project_up: float32 [768, 3072], P('dp', 'tensor'), may hold values from 7.064254e-09 to 2.8257016e-08
- second_project_down: float32 [3072, 768], P('tensor', 'dp'), may hold values from 7.064254e-09 to 2.8257016e-08
- second_norms: float32 [4, 768], P(None, 'dp'), may hold values from 6.357829e-08 to 2.5431316e-07
Outputs:
- block_out: bfloat16 [11776, 768], P(('dp', 'tensor'))
- grad_tokens: bfloat16 [11776, 768], P(('dp', 'tensor'))
- grad_attend_in: float32 [3, 768, 768], P(None, 'dp', 'tensor')
- grad_attend_out: float32 [768, 768], P('tensor', 'dp')
- grad_project_up: float32 [768, 3072], P('dp', 'tensor')
- grad_project_down: float32 [3072, 768], P('tensor', 'dp')
- grad_norms: float32 [4, 768], P(None, 'dp')
- mean_attend_in: float32 [3, 768, 768], P(None, 'dp', 'tensor')
- mean_attend_out: float32 [768, 768], P('tensor', 'dp')
- mean_project_up: float32 [768, 3072], P('dp', 'tensor')
- mean_project_down: float32 [3072, 768], P('tensor', 'dp')
- mean_norms: float32 [4, 768], P(None, 'dp')
- square_attend_in: float32 [3, 768, 768], P(None, 'dp', 'tensor')
- square_attend_out: float32 [768, 768], P('tensor', 'dp')
- square_project_up: float32 [768, 3072], P('dp', 'tensor')
- square_project_down: float32 [3072, 768], P('tensor', 'dp')
- square_norms: float32 [4, 768], P(None, 'dp')
- master_attend_in: float32 [3, 768, 768], P(None, 'dp', 'tensor')
- master_attend_out: float32 [768, 768], P('tensor', 'dp')
- master_project_up: float32 [768, 3072], P('dp', 'tensor')
- master_project_down: float32 [3072, 768], P('tensor', 'dp')
- master_norms: float32 [4, 768], P(None, 'dp')
- copy_attend_in: bfloat16 [3, 768, 768], P(None, 'dp', 'tensor')
- copy_attend_out: bfloat16 [768, 768], P('tensor', 'dp')
- copy_project_up: bfloat16 [768, 3072], P('dp', 'tensor')
- copy_project_down: bfloat16 [3072, 768], P('tensor', 'dp')
- grad_norm_total: float32 [1], replicated
The draws below stay inside these ranges and needn't reach their ends.
Inputs may be any that keep to these rules, and one draw needn't show every extreme that they name: `horizons`: horizon of each clip in frames; some clip has 30.
All inputs are finite; a program needn't handle non-finite values.
Results may differ from the reference program's by a relative error of at most 0.017.
Values may be sent and summed in bfloat16 or wider, within the bound.
No kernel may reach another device: no remote copies, remote signals or barrier semaphores. Data moves between devices by JAX's collectives and lax.ppermute only.
A program may use at most 128 MiB of HBM per device.

```python
import math
import jax
import jax.numpy as jnp
from jax import lax

D = 768
HEADS = 12
HS = 64
FF = 3072
CTX = 256
FRAME = 16
HMIN = 4
HMAX = 30
CAP = 736
CLIPS_DEV = 2
CLIPS = 16
TOKENS = 11776
N_DP = 8


def draw_horizons(key, part):
    first_key, second_key, place_key = jax.random.split(jax.random.fold_in(key, 11), 3)
    draw_one = jax.random.randint(first_key, (CLIPS,), 0, HMAX - HMIN + 1, dtype=jnp.int32)
    draw_two = jax.random.randint(second_key, (CLIPS,), 0, HMAX - HMIN + 1, dtype=jnp.int32)
    frames = HMIN + jnp.minimum(draw_one, draw_two)
    longest = jax.random.randint(place_key, (), 0, CLIPS, dtype=jnp.int32)
    places = jnp.arange(CLIPS, dtype=jnp.int32)
    return jnp.where(places == longest, HMAX, frames).astype(jnp.int32)


def levels(rng, extent, shards, low, largest):
    def one(axis_at, shards_of):
        steps = jax.random.uniform(jax.random.fold_in(jax.random.fold_in(rng, 6), axis_at), (shards_of,), jnp.float32, low / len(shards), largest / len(shards))
        return jnp.repeat(jnp.exp(steps), extent[axis_at] // shards_of).reshape((-1,) + (1,) * (len(extent) - axis_at - 1))

    loudness = one(*shards[0])
    for cut in shards[1:]:
        loudness = loudness * one(*cut)
    return loudness


def gaussian(rng, shape, width, reach, pieces=(), held_as=jnp.bfloat16):
    entries = width * jax.random.normal(rng, shape, jnp.float32)
    if pieces:
        entries = entries * levels(rng, shape, pieces, -0.22, 0.18)
    return jnp.clip(entries, -reach, reach).astype(held_as)


def setup_inputs(seed: int = 0) -> dict:
    key_of = jax.random.split(jax.random.key(seed), 21)
    return {
        "tokens": gaussian(key_of[0], (TOKENS, D), 1.0, 6.0, ((0, 32),)),
        "horizons": draw_horizons(jax.random.fold_in(key_of[20], 71), 0),
        "cotangent": gaussian(key_of[2], (TOKENS, D), 1.0, 6.0, ((0, 32),)),
        "step_number": jax.random.randint(key_of[3], (1,), 2, 21).astype(jnp.int32),
        "attend_in": gaussian(key_of[4], (3, D, D), D ** -0.5, 0.21875, ((1, 8), (2, 4)), jnp.float32),
        "attend_out": gaussian(key_of[5], (D, D), (D // 64) ** -0.5, 1.75, ((0, 4), (1, 8)), jnp.float32),
        "project_up": gaussian(key_of[6], (D, FF), D ** -0.5, 0.21875, ((0, 8), (1, 4)), jnp.float32),
        "project_down": gaussian(key_of[7], (FF, D), FF ** -0.5, 0.109375, ((0, 4), (1, 8)), jnp.float32),
        "norm_gains": jnp.clip(1.0 + 0.18 * jax.random.normal(key_of[8], (2, D), jnp.float32), 0.1, 1.9),
        "norm_biases": gaussian(key_of[9], (2, D), 0.3, 1.8, (), jnp.float32),
        "first_attend_in": gaussian(key_of[10], (3, D, D), (0.11 / (12 * D * D) ** 0.5), 0.0002480802, ((1, 8), (2, 4)), jnp.float32),
        "first_attend_out": gaussian(key_of[11], (D, D), (0.11 / (12 * D * D) ** 0.5), 0.0002480802, ((0, 4), (1, 8)), jnp.float32),
        "first_project_up": gaussian(key_of[12], (D, FF), (0.11 / (12 * D * D) ** 0.5), 0.0002480802, ((0, 8), (1, 4)), jnp.float32),
        "first_project_down": gaussian(key_of[13], (FF, D), (0.11 / (12 * D * D) ** 0.5), 0.0002480802, ((0, 4), (1, 8)), jnp.float32),
        "first_norms": gaussian(key_of[14], (4, D), (0.33 / (12 * D * D) ** 0.5), 0.0007442406, ((1, 8),), jnp.float32),
        "second_attend_in": jnp.clip(jnp.exp(math.log(2.8257016282395853e-08) - 1.3862944 * jax.random.uniform(key_of[15], (3, D, D), jnp.float32) ** levels(key_of[15], (3, D, D), ((1, 8), (2, 4)), -0.2, 0.2)), 7.064254070598963e-09, 2.8257016282395853e-08),
        "second_attend_out": jnp.clip(jnp.exp(math.log(2.8257016282395853e-08) - 1.3862944 * jax.random.uniform(key_of[16], (D, D), jnp.float32) ** levels(key_of[16], (D, D), ((0, 4), (1, 8)), -0.2, 0.2)), 7.064254070598963e-09, 2.8257016282395853e-08),
        "second_project_up": jnp.clip(jnp.exp(math.log(2.8257016282395853e-08) - 1.3862944 * jax.random.uniform(key_of[17], (D, FF), jnp.float32) ** levels(key_of[17], (D, FF), ((0, 8), (1, 4)), -0.2, 0.2)), 7.064254070598963e-09, 2.8257016282395853e-08),
        "second_project_down": jnp.clip(jnp.exp(math.log(2.8257016282395853e-08) - 1.3862944 * jax.random.uniform(key_of[18], (FF, D), jnp.float32) ** levels(key_of[18], (FF, D), ((0, 4), (1, 8)), -0.2, 0.2)), 7.064254070598963e-09, 2.8257016282395853e-08),
        "second_norms": jnp.clip(jnp.exp(math.log(2.5431316430513107e-07) - 1.3862944 * jax.random.uniform(key_of[19], (4, D), jnp.float32) ** levels(key_of[19], (4, D), ((1, 8),), -0.2, 0.2)), 6.357829107628277e-08, 2.5431316430513107e-07),
    }


@jax.custom_vjp
def low(v):
    return lax.optimization_barrier(v.astype(jnp.bfloat16)).astype(jnp.float32)

@jax.custom_vjp
def low_back(v):
    return v

def low_keep(v):
    return (low(v), None)

def low_pass(kept, grad):
    return (grad,)

def back_keep(v):
    return (v, None)

def back_low(kept, grad):
    return (low(grad),)
low.defvjp(low_keep, low_pass)
low_back.defvjp(back_keep, back_low)
norm_eps = 1e-05
beta_one = 0.9
beta_two = 0.95
adam_eps = 1e-08
rate_matrix = 0.05
rate_out = 0.4
rate_norm = 0.4
decay_weight = 0.1
clip_limit = 1.0
neg_fill = -1e+30

def layer_norm(rows_in, gain, shift):
    center = lax.optimization_barrier(jnp.mean(rows_in, axis=-1, keepdims=True))
    centred = rows_in - center
    spread = lax.optimization_barrier(jnp.mean(centred * centred, axis=-1, keepdims=True))
    return centred * lax.rsqrt(spread + norm_eps) * gain + shift

def attend(member):
    queries, key_rows, value_rows, length = member
    clip_span = queries.shape[0]
    raw = jnp.einsum('qhd,khd->hqk', queries, key_rows, precision=lax.Precision.HIGHEST) * HS ** (-0.5)
    scores = low_back(raw)
    places = jnp.arange(clip_span, dtype=jnp.int32)
    allowed = (places[None, :] <= places[:, None]) & (places[None, :] < length)
    scores = jnp.where(allowed[None], scores, neg_fill)
    chances = jax.nn.softmax(scores, axis=-1)
    return jnp.einsum('hqk,khd->qhd', low(chances), value_rows, precision=lax.Precision.HIGHEST)

def block_forward(stream, clip_lengths, attend_in, attend_out, project_up, project_down, norm_gains, norm_biases):
    highest = lax.Precision.HIGHEST
    low_in = low(attend_in)
    normed = low(layer_norm(stream, norm_gains[0], norm_biases[0]))
    clip_count = clip_lengths.shape[0]
    parts = []
    for which in range(3):
        projected = low(low_back(jnp.dot(normed, low_in[which], precision=highest)))
        parts.append(projected.reshape(clip_count, CAP, HEADS, HS))
    mixture = lax.map(jax.checkpoint(attend), (parts[0], parts[1], parts[2], clip_lengths))
    mixture = low(low_back(mixture.reshape(clip_count * CAP, D)))
    residual = stream + low_back(jnp.dot(mixture, low(attend_out), precision=highest))
    normed_two = low(layer_norm(residual, norm_gains[1], norm_biases[1]))
    hidden = low_back(jnp.dot(normed_two, low(project_up), precision=highest))
    active = low(jax.nn.gelu(hidden, approximate=True))
    return residual + low_back(jnp.dot(active, low(project_down), precision=highest))

def adam_step(weight, grad, first, second, rate, decay, correct_one, correct_two):
    mean_new = beta_one * first + (1.0 - beta_one) * grad
    square_new = beta_two * second + (1.0 - beta_two) * grad * grad
    direction = mean_new / correct_one / (jnp.sqrt(square_new / correct_two) + adam_eps)
    return (mean_new, square_new, weight - rate * (direction + decay * weight))

def reference(tokens, horizons, cotangent, step_number, attend_in, attend_out, project_up, project_down, norm_gains, norm_biases, first_attend_in, first_attend_out, first_project_up, first_project_down, first_norms, second_attend_in, second_attend_out, second_project_up, second_project_down, second_norms):
    group_rows = CLIPS_DEV * CAP
    weights = (attend_in, attend_out, project_up, project_down, norm_gains, norm_biases)

    def one_group(carry, member):
        stream_in, frames, grad_in = member
        clip_lengths = (CTX + FRAME * frames).astype(jnp.int32)
        stream = stream_in.astype(jnp.float32)
        places = jnp.arange(group_rows, dtype=jnp.int32)
        limits = clip_lengths[places // CAP]
        live = (places % CAP < limits).astype(jnp.float32)
        grad_out = grad_in.astype(jnp.float32) * live[:, None]

        def forward_fn(stream_x, w_one, w_two, w_three, w_four, gains, shifts):
            return block_forward(stream_x, clip_lengths, w_one, w_two, w_three, w_four, gains, shifts)
        result, pullback = jax.vjp(forward_fn, stream, *weights)
        grads = pullback(grad_out)
        carry = tuple((total + part for total, part in zip(carry, grads[1:])))
        return (carry, (result.astype(jnp.bfloat16), grads[0].astype(jnp.bfloat16)))
    zeros = tuple((jnp.zeros(weight.shape, jnp.float32) for weight in weights))
    totals, outputs = lax.scan(one_group, zeros, (tokens.reshape(N_DP, group_rows, D), horizons.reshape(N_DP, CLIPS_DEV), cotangent.reshape(N_DP, group_rows, D)))
    block_out = outputs[0].reshape(TOKENS, D)
    grad_tokens = outputs[1].reshape(TOKENS, D)
    matrix_grads = totals[:4]
    norm_grad = jnp.concatenate([totals[4], totals[5]], axis=0)
    squares = norm_grad * norm_grad
    total_sq = jnp.sum(squares)
    for grad in matrix_grads:
        total_sq = total_sq + jnp.sum(grad * grad)
    grad_total = jnp.sqrt(total_sq)
    factor = jnp.minimum(1.0, clip_limit / grad_total)
    clipped = [grad * factor for grad in matrix_grads]
    norm_clipped = norm_grad * factor
    step_count = step_number[0].astype(jnp.float32)
    correct_one = 1.0 - jnp.exp(step_count * jnp.log(beta_one))
    correct_two = 1.0 - jnp.exp(step_count * jnp.log(beta_two))
    masters = (attend_in, attend_out, project_up, project_down)
    firsts = (first_attend_in, first_attend_out, first_project_up, first_project_down)
    seconds = (second_attend_in, second_attend_out, second_project_up, second_project_down)
    matrix_rates = (rate_matrix, rate_out, rate_matrix, rate_matrix)
    means = []
    squares_new = []
    updated = []
    for weight, grad, first, second, rate in zip(masters, clipped, firsts, seconds, matrix_rates):
        mean_new, square_new, weight_new = adam_step(weight, grad, first, second, rate, decay_weight, correct_one, correct_two)
        means.append(mean_new)
        squares_new.append(square_new)
        updated.append(weight_new)
    norm_params = jnp.concatenate([norm_gains, norm_biases], axis=0)
    norm_mean, norm_square, norm_new = adam_step(norm_params, norm_clipped, first_norms, second_norms, rate_norm, 0.0, correct_one, correct_two)
    return (block_out, grad_tokens, clipped[0], clipped[1], clipped[2], clipped[3], norm_clipped, means[0], means[1], means[2], means[3], norm_mean, squares_new[0], squares_new[1], squares_new[2], squares_new[3], norm_square, updated[0], updated[1], updated[2], updated[3], norm_new, updated[0].astype(jnp.bfloat16), updated[1].astype(jnp.bfloat16), updated[2].astype(jnp.bfloat16), updated[3].astype(jnp.bfloat16), grad_total.reshape(1))
```

```python
import jax
import jax.numpy as jnp
from jax import lax
from jax.sharding import Mesh, PartitionSpec as P

HS = 64
CTX = 256
FRAME = 16

norm_eps = 1e-05
beta_one = 0.9
beta_two = 0.95
adam_eps = 1e-08
rate_matrix = 0.05
rate_out = 0.4
rate_norm = 0.4
decay_weight = 0.1
clip_limit = 1.0
neg_fill = -1e30
BF = jnp.bfloat16
F32 = jnp.float32


def layer_norm(rows_in, gain, shift):
    center = jnp.mean(rows_in, axis=-1, keepdims=True)
    centred = rows_in - center
    spread = jnp.mean(centred * centred, axis=-1, keepdims=True)
    return centred * lax.rsqrt(spread + norm_eps) * gain + shift


def gelu_tanh(values):
    return jax.nn.gelu(values, approximate=True)


def dot_nn(left, right):
    return lax.dot_general(left, right, (((1,), (0,)), ((), ())), preferred_element_type=F32)


def dot_nt(left, right):
    return lax.dot_general(left, right, (((1,), (1,)), ((), ())), preferred_element_type=F32)


def dot_tn(left, right):
    return lax.dot_general(left, right, (((0,), (0,)), ((), ())), preferred_element_type=F32)


def ring(count, step):
    return [(place, (place + step) % count) for place in range(count)]


def hop(value, axis, count, step):
    return lax.ppermute(value, axis, ring(count, step))


def axis_gather(block, axis, count):
    blocks = [block]
    for _ in range(count - 1):
        blocks.append(hop(blocks[-1], axis, count, 1))
    return blocks


def axis_scatter(parts, axis, count):
    total = parts[count - 1]
    for place in range(count - 2, -1, -1):
        moved = hop(total.astype(BF), axis, count, count - 1)
        total = moved.astype(F32) + parts[place].astype(F32)
    return total


def clip_mask(clip_span, length):
    places = jnp.arange(clip_span, dtype=jnp.int32)
    return (places[None, :] <= places[:, None]) & (places[None, :] < length)


def clip_scores(queries, key_rows, length):
    scale = queries.shape[-1] ** (-0.5)
    scores = jnp.einsum("qhd,khd->hqk", queries, key_rows, preferred_element_type=F32) * scale
    return jnp.where(clip_mask(queries.shape[0], length)[None], scores, neg_fill)


def attend_clip(queries, key_rows, value_rows, length):
    scores = clip_scores(queries, key_rows, length)
    highest = jnp.max(scores, axis=-1, keepdims=True)
    exponent = jnp.exp(scores - highest)
    totals = jnp.sum(exponent, axis=-1, keepdims=True)
    chances = (exponent / totals).astype(BF)
    mixture = jnp.einsum("hqk,khd->qhd", chances, value_rows, preferred_element_type=F32)
    return (mixture.astype(BF), highest + jnp.log(totals))


def attend_back(queries, key_rows, value_rows, length, log_total, grad_mix):
    scale = queries.shape[-1] ** (-0.5)
    chances = jnp.exp(clip_scores(queries, key_rows, length) - log_total)
    rounded = chances.astype(BF)
    grad_chances = jnp.einsum("qhd,khd->hqk", grad_mix, value_rows, preferred_element_type=F32)
    inner_sum = jnp.sum(chances * grad_chances, axis=-1, keepdims=True)
    grad_scores = (chances * (grad_chances - inner_sum)).astype(BF)
    grad_query = jnp.einsum("hqk,khd->qhd", grad_scores, key_rows, preferred_element_type=F32)
    grad_key = jnp.einsum("hqk,qhd->khd", grad_scores, queries, preferred_element_type=F32)
    grad_value = jnp.einsum("hqk,qhd->khd", rounded, grad_mix, preferred_element_type=F32)
    return (
        (grad_query * scale).astype(BF),
        (grad_key * scale).astype(BF),
        grad_value.astype(BF),
    )


def adam_step(weight, grad, first, second, rate, decay, correct_one, correct_two):
    mean_new = beta_one * first + (1.0 - beta_one) * grad
    square_new = beta_two * second + (1.0 - beta_two) * grad * grad
    direction = mean_new / correct_one / (jnp.sqrt(square_new / correct_two) + adam_eps)
    return (mean_new, square_new, weight - rate * (direction + decay * weight))


def split_axis(count):
    parts = []
    while count % 4 == 0:
        parts.append(4)
        count //= 4
    if count > 1:
        parts.append(count)
    return parts


class Plan:
    def __init__(self, mesh):
        self.grid = split_axis(mesh.shape["dp"])
        self.names = ["d%d" % place for place in range(len(self.grid))]
        self.clips = mesh.shape["tensor"] // 2
        self.dp = tuple(self.names)
        self.all = self.dp + ("clip", "core")
        self.mesh = Mesh(
            mesh.devices.reshape(tuple(self.grid) + (self.clips, 2)), self.all
        )

    def order(self, width, block):
        slot = jnp.arange(width, dtype=jnp.int32)
        half = block // 2
        inner = slot % half
        rest = slot // half
        home = jnp.zeros_like(slot)
        weight = 1
        moved = []
        for name, count in zip(self.names, self.grid):
            moved.append((lax.axis_index(name) - rest % count) % count)
            rest = rest // count
        for place in range(len(self.grid) - 1, -1, -1):
            home = home + moved[place] * weight
            weight = weight * self.grid[place]
        return home * block + rest * half + inner

    def gather(self, block):
        half = block.shape[0] // 2
        lead = axis_gather(block, self.names[0], self.grid[0])
        first = jnp.concatenate([piece[:half] for piece in lead], axis=0)
        second = jnp.concatenate([piece[half:] for piece in lead], axis=0)
        rest = list(zip(self.names[1:], self.grid[1:]))
        for name, count in rest:
            first = jnp.concatenate(axis_gather(first, name, count), axis=0)
        first = axis_gather(first, "clip", self.clips)
        second = axis_gather(second, "clip", self.clips)
        sizes = second[0].shape[0]
        packed = jnp.concatenate(second, axis=0)
        for name, count in rest:
            pieces = axis_gather(packed, name, count)
            parts = [
                jnp.concatenate([piece[at * sizes : (at + 1) * sizes] for piece in pieces], axis=0)
                for at in range(self.clips)
            ]
            sizes = sizes * count
            packed = jnp.concatenate(parts, axis=0)
        return [
            jnp.concatenate([first[at], packed[at * sizes : (at + 1) * sizes]], axis=0)
            for at in range(self.clips)
        ]

    def scatter(self, parts):
        half = parts[0].shape[0] // 2
        first = axis_scatter([part[:half] for part in parts], "clip", self.clips)
        second = [part[half:] for part in parts]
        rest = list(zip(self.names[1:], self.grid[1:]))
        for name, count in reversed(rest):
            first = first.astype(BF)
            size = first.shape[0] // count
            first = axis_scatter(
                [first[at * size : (at + 1) * size] for at in range(count)], name, count
            )
            size = second[0].shape[0] // count
            joined = [
                jnp.concatenate([part[at * size : (at + 1) * size] for part in second], axis=0)
                for at in range(count)
            ]
            total = axis_scatter(joined, name, count).astype(BF)
            second = [total[at * size : (at + 1) * size] for at in range(self.clips)]
        second = axis_scatter(second, "clip", self.clips)
        first = first.astype(BF)
        second = second.astype(BF)
        count = self.grid[0]
        size = first.shape[0] // count
        joined = [
            jnp.concatenate(
                [first[at * size : (at + 1) * size], second[at * size : (at + 1) * size]], axis=0
            )
            for at in range(count)
        ]
        return axis_scatter(joined, self.names[0], count)

    def total(self, value):
        for name, count in zip(
            ("core", "clip") + tuple(reversed(self.names)), [2, self.clips] + self.grid[::-1]
        ):
            moved = value
            summed = value
            for _ in range(count - 1):
                moved = hop(moved, name, count, 1)
                summed = summed + moved
            value = summed
        return value


def swap(value):
    return lax.ppermute(value, "core", [(0, 1), (1, 0)])


def on_device(
    plan,
    tokens,
    horizons,
    cotangent,
    step_number,
    attend_in,
    attend_out,
    project_up,
    project_down,
    norm_gains,
    norm_biases,
    first_attend_in,
    first_attend_out,
    first_project_up,
    first_project_down,
    first_norms,
    second_attend_in,
    second_attend_out,
    second_project_up,
    second_project_down,
    second_norms,
):
    core = lax.axis_index("core")
    rows, width = tokens.shape
    block, low_cols = attend_in.shape[1], attend_in.shape[2]
    span = 2 * rows
    heads_cols = plan.clips * low_cols
    local_heads = heads_cols // HS

    in_block = jnp.transpose(attend_in, (1, 0, 2)).reshape(block, 3 * low_cols)
    shard_attn = jnp.concatenate([in_block, attend_out.T], axis=1).astype(BF)
    shard_up = project_up.astype(BF)
    shard_down = project_down.T.astype(BF)
    whole_attn = plan.gather(shard_attn)
    whole_up = plan.gather(shard_up)
    whole_down = plan.gather(shard_down)
    low_in = jnp.concatenate([part[:, : 3 * low_cols] for part in whole_attn], axis=1)
    low_out = jnp.concatenate([part[:, 3 * low_cols :] for part in whole_attn], axis=1)
    low_up = jnp.concatenate(whole_up, axis=1)
    low_down = jnp.concatenate(whole_down, axis=1)
    both_out = jnp.concatenate([low_out, swap(low_out)], axis=1)

    order = plan.order(width, block)
    chooser = (jnp.arange(width, dtype=jnp.int32)[:, None] == order[None, :]).astype(BF)
    clip = lax.axis_index("clip")
    length = CTX + FRAME * lax.dynamic_index_in_dim(horizons, clip, 0, keepdims=False)

    def whole_clip(own):
        other = swap(own)
        return jnp.where(
            core == 0,
            jnp.concatenate([own, other], axis=0),
            jnp.concatenate([other, own], axis=0),
        )

    def own_rows(whole):
        return lax.dynamic_slice_in_dim(whole, core * rows, rows, 0)

    def other_rows(whole):
        return lax.dynamic_slice_in_dim(whole, (1 - core) * rows, rows, 0)

    stream_low = whole_clip(dot_nn(tokens, chooser).astype(BF))
    grad_low = whole_clip(dot_nn(cotangent, chooser).astype(BF))
    norms = jnp.concatenate([norm_gains, norm_biases], axis=0)
    norms_own = lax.dot_general(
        norms,
        chooser.astype(F32),
        (((1,), (0,)), ((), ())),
        precision=lax.Precision.HIGHEST,
        preferred_element_type=F32,
    )
    gain_one, gain_two, shift_one, shift_two = [norms_own[at] for at in range(4)]
    live = (jnp.arange(span, dtype=jnp.int32) < length).astype(F32)
    grad_stream = grad_low.astype(F32) * live[:, None]
    grad_rows = grad_stream.astype(BF)

    stream = stream_low.astype(F32)
    normed = layer_norm(stream, gain_one, shift_one).astype(BF)
    projected = dot_nn(normed, low_in).astype(BF)
    parts = projected.reshape(span, plan.clips, 3, low_cols)
    head_parts = [
        parts[:, :, which].reshape(span, local_heads, HS) for which in range(3)
    ]
    mixture, log_total = attend_clip(head_parts[0], head_parts[1], head_parts[2], length)
    mixture = mixture.reshape(span, heads_cols)
    both = jnp.concatenate([mixture, swap(mixture)], axis=1)
    residual = stream + dot_nt(both, both_out)
    normed_two = layer_norm(residual, gain_two, shift_two).astype(BF)
    hidden = dot_nn(normed_two, low_up)
    active = gelu_tanh(hidden).astype(BF)

    grad_active = dot_nn(grad_rows, low_down)
    unused_gelu, gelu_back = jax.vjp(gelu_tanh, hidden)
    grad_hidden = gelu_back(grad_active)[0].astype(BF)
    ff = low_up.shape[1] // plan.clips
    grad_down = dot_tn(grad_rows, active).astype(BF)
    sum_down = plan.scatter([grad_down[:, at * ff : (at + 1) * ff] for at in range(plan.clips)])
    grad_up = dot_tn(normed_two, grad_hidden).astype(BF)
    sum_up = plan.scatter([grad_up[:, at * ff : (at + 1) * ff] for at in range(plan.clips)])
    share_two = dot_nt(grad_hidden, low_up).astype(BF)
    grad_normed_two = share_two.astype(F32) + swap(share_two).astype(F32)
    unused_norm, norm_back_two = jax.vjp(layer_norm, residual, gain_two, shift_two)
    grad_from_norm, gain_grad_two, shift_grad_two = norm_back_two(grad_normed_two)
    grad_residual = grad_stream + grad_from_norm
    grad_rows_two = grad_residual.astype(BF)

    share_out = dot_nt(active, low_down).astype(BF)
    branch = own_rows(share_out).astype(F32) + swap(other_rows(share_out)).astype(F32)
    result = (own_rows(residual) + branch).astype(BF)
    block_out = dot_nt(result, chooser).astype(BF)

    grad_mixture = dot_nn(grad_rows_two, low_out).astype(BF)
    grad_merge = dot_tn(grad_rows_two, mixture).astype(BF)
    grad_query, grad_key, grad_value = attend_back(
        head_parts[0],
        head_parts[1],
        head_parts[2],
        length,
        log_total,
        grad_mixture.reshape(span, local_heads, HS),
    )
    grad_heads = jnp.stack(
        [g.reshape(span, plan.clips, low_cols) for g in (grad_query, grad_key, grad_value)], axis=2
    ).reshape(span, 3 * heads_cols)
    grad_inproj = dot_tn(normed, grad_heads).astype(BF)
    wide = 3 * low_cols
    sum_attn = plan.scatter(
        [
            jnp.concatenate(
                [
                    grad_inproj[:, at * wide : (at + 1) * wide],
                    grad_merge[:, at * low_cols : (at + 1) * low_cols],
                ],
                axis=1,
            )
            for at in range(plan.clips)
        ]
    )
    share_one = dot_nt(grad_heads, low_in).astype(BF)
    grad_normed = own_rows(share_one).astype(F32) + swap(other_rows(share_one)).astype(F32)
    unused_first, norm_back_one = jax.vjp(layer_norm, own_rows(stream), gain_one, shift_one)
    grad_input_norm, gain_grad_one, shift_grad_one = norm_back_one(grad_normed)
    grad_tokens_own = (own_rows(grad_residual) + grad_input_norm).astype(BF)
    grad_tokens = dot_nt(grad_tokens_own, chooser).astype(BF)

    norm_part = jnp.stack(
        [gain_grad_one, 0.5 * gain_grad_two, shift_grad_one, 0.5 * shift_grad_two]
    )
    norm_part = lax.dot_general(
        norm_part,
        chooser.astype(F32),
        (((1,), (1,)), ((), ())),
        precision=lax.Precision.HIGHEST,
        preferred_element_type=F32,
    )
    norm_whole = plan.total(norm_part)

    local_squares = (
        jnp.sum(sum_attn * sum_attn) + jnp.sum(sum_up * sum_up) + jnp.sum(sum_down * sum_down)
    )
    square_sum = plan.total(jnp.full((8, 128), local_squares, F32))[0, 0]
    grad_total = jnp.sqrt(square_sum + jnp.sum(norm_whole * norm_whole))
    factor = jnp.minimum(1.0, clip_limit / grad_total)

    index = jnp.int32(0)
    for name, count in zip(plan.names, plan.grid):
        index = index * count + lax.axis_index(name)

    def own_norm(whole):
        return lax.dynamic_slice_in_dim(whole, index * block, block, 1)

    owned = (
        jnp.transpose(sum_attn[:, :wide].reshape(block, 3, low_cols), (1, 0, 2)),
        sum_attn[:, wide:].T,
        sum_up,
        sum_down.T,
    )
    clipped = [grad * factor for grad in owned]
    norm_clipped = own_norm(norm_whole) * factor
    step_count = step_number[0].astype(F32)
    correct_one = 1.0 - jnp.exp(step_count * jnp.log(beta_one))
    correct_two = 1.0 - jnp.exp(step_count * jnp.log(beta_two))
    masters = (attend_in, attend_out, project_up, project_down)
    firsts = (first_attend_in, first_attend_out, first_project_up, first_project_down)
    seconds = (second_attend_in, second_attend_out, second_project_up, second_project_down)
    matrix_rates = (rate_matrix, rate_out, rate_matrix, rate_matrix)
    means = []
    squares_new = []
    updated = []
    for weight, grad, first, second, rate in zip(masters, clipped, firsts, seconds, matrix_rates):
        mean_new, square_new, weight_new = adam_step(
            weight, grad, first, second, rate, decay_weight, correct_one, correct_two
        )
        means.append(mean_new)
        squares_new.append(square_new)
        updated.append(weight_new)
    norm_mean, norm_square, norm_new = adam_step(
        own_norm(norms),
        norm_clipped,
        first_norms,
        second_norms,
        rate_norm,
        0.0,
        correct_one,
        correct_two,
    )
    return (
        block_out,
        grad_tokens,
        clipped[0],
        clipped[1],
        clipped[2],
        clipped[3],
        norm_clipped,
        means[0],
        means[1],
        means[2],
        means[3],
        norm_mean,
        squares_new[0],
        squares_new[1],
        squares_new[2],
        squares_new[3],
        norm_square,
        updated[0],
        updated[1],
        updated[2],
        updated[3],
        norm_new,
        updated[0].astype(BF),
        updated[1].astype(BF),
        updated[2].astype(BF),
        updated[3].astype(BF),
        grad_total.reshape(1),
    )


def solution(mesh):
    plan = Plan(mesh)
    dp = plan.dp
    both = ("clip", "core")
    rows = P(plan.all, None)
    matrices = (P(None, dp, both), P(both, dp), P(dp, both), P(both, dp))
    norms = P(None, dp)
    return jax.shard_map(
        lambda *args: on_device(plan, *args),
        mesh=plan.mesh,
        in_specs=(rows, P(dp), rows, P())
        + matrices
        + (P(), P())
        + matrices
        + (norms,)
        + matrices
        + (norms,),
        out_specs=(rows, rows)
        + (matrices + (norms,)) * 4
        + matrices
        + (P(),),
        check_vma=False,
    )
```
